512 devices in a mesh: dp: 64 (over y, z), mp: 8 (over x, core).
Axes of the slice: x: 4, y: 8, z: 8, core: 2. Of those that a mesh axis runs over, the one named last changes fastest.
Arguments:
- activations: bfloat16 [32768, 8192], P('dp', 'mp'), may hold values from -6 to 6
- out_grads: bfloat16 [32768, 8192], P('dp', 'mp'), may hold values from -0.09375 to 0.09375
- basis: bfloat16 [8192, 1024], P('mp'), may hold values from -0.0625 to 0.0625
- moment1: float32 [8192, 1024], P(('mp', 'dp')), may hold values from -1.5 to 1.5
- moment2: float32 [8192, 1024], P(('mp', 'dp')), may hold values from 0.0005 to 0.005
Outputs:
- new_first: float32 [8192, 1024], P(('mp', 'dp'))
- new_second: float32 [8192, 1024], P(('mp', 'dp'))
- update: bfloat16 [8, 1024, 8192], P(None, 'dp', 'mp')
The draws below stay inside these ranges and needn't reach their ends.
All inputs are finite; a program needn't handle non-finite values.
Results may differ from the reference program's by a relative error of at most 0.0055.
Values may be sent and summed in bfloat16 or wider, within the bound.
A program may use at most 64 MiB of HBM per device.

```python
import math
import jax
import jax.numpy as jnp
from jax import lax

D = 8192
NOUT = 8192
R = 1024
STEP = 100
TOKENS = 32768
N_MP = 8


def raised(array, rng, source, target, blocks, factor):
    owner, partner = [(jnp.arange(array.shape[axis_at]) // (array.shape[axis_at] // blocks)).reshape([-1 if axis == axis_at else 1 for axis in range(array.ndim)]) for axis_at in (source, target)]
    chosen = jax.random.permutation(rng, blocks)[partner]
    strong = (owner == chosen) | (owner == (partner + blocks // 2) % blocks)
    return jnp.where(strong, factor * array, array)


def shard_levels(stream_key, shape, pieces, low, high):
    loudness, own = 1.0, jax.random.fold_in(stream_key, 6)
    for position, shards_of in pieces:
        draws = jnp.exp(jax.random.uniform(jax.random.fold_in(own, position), (shards_of,), jnp.float32, low / len(pieces), high / len(pieces)))
        loudness = loudness * jnp.repeat(draws, shape[position] // shards_of).reshape([-1 if axis == position else 1 for axis in range(len(shape))])
    return loudness


def scatter_about(rng, extent, deviation, limit, pieces=(), kind=jnp.bfloat16):
    level = shard_levels(rng, extent, pieces, -0.22, 0.18) if pieces else 1.0
    array = jax.random.normal(rng, extent, jnp.float32) * deviation * level
    return jnp.minimum(jnp.maximum(array, -limit), limit).astype(kind)


def gaussian_with(own_key, shape, width, limit, split, heavy, kind=jnp.bfloat16):
    result = width * jax.random.normal(own_key, shape, jnp.float32)
    if split:
        result = result * shard_levels(own_key, shape, split, -0.22, 0.18)
    return jnp.clip(raised(result, jax.random.fold_in(own_key, 3), *heavy), -limit, limit).astype(kind)


def setup_inputs(seed: int = 0) -> dict:
    key_of = jax.random.split(jax.random.key(seed), 6)
    activations = scatter_about(key_of[0], (TOKENS, D), 1.0, 6.0, ((0, 64), (1, 8)))
    out_grads = gaussian_with(key_of[1], (TOKENS, NOUT), TOKENS ** -0.5, 0.09375, ((0, 64), (1, 8)), (0, 1, 64, 4.0))
    basis = scatter_about(key_of[2], (D, R), D ** -0.5, 0.0625, ((0, 8),))
    moment1 = scatter_about(key_of[3], (NOUT, R), 0.1, 1.5, ((0, 512),), jnp.float32)
    moment2 = jnp.clip(jnp.exp(math.log(0.005) - 2.30258502 * jax.random.uniform(key_of[4], (NOUT, R), jnp.float32) ** shard_levels(key_of[4], (NOUT, R), ((0, 512),), -0.2, 0.2)), 0.0005, 0.005)
    return {"activations": activations, "out_grads": out_grads, "basis": basis, "moment1": moment1, "moment2": moment2}


beta_first = 0.9
beta_second = 0.999
epsilon = 1e-08

def reference(activations, out_grads, basis, moment1, moment2):
    highest = lax.Precision.HIGHEST
    basis_wide = basis.astype(jnp.float32)
    token_rank = jnp.dot(activations.astype(jnp.float32), basis_wide, precision=highest, preferred_element_type=jnp.float32).astype(jnp.bfloat16)
    reduced = jnp.dot(out_grads.astype(jnp.float32).T, token_rank.astype(jnp.float32), precision=highest, preferred_element_type=jnp.float32)
    new_first = beta_first * moment1 + (1.0 - beta_first) * reduced
    new_second = beta_second * moment2 + (1.0 - beta_second) * reduced * reduced
    bias_first = 1.0 - beta_first ** STEP
    bias_second = 1.0 - beta_second ** STEP
    normed = (new_first / bias_first / (jnp.sqrt(new_second / bias_second) + epsilon)).astype(jnp.bfloat16)
    full = jnp.dot(normed.astype(jnp.float32), basis_wide.T, precision=highest, preferred_element_type=jnp.float32).astype(jnp.bfloat16)
    update = full.reshape(N_MP, NOUT // N_MP, D)
    return (new_first, new_second, update)
```

```python
import jax
import jax.numpy as jnp
from jax import lax
from jax.experimental import pallas as pl
from jax.experimental.pallas import tpu as pltpu
from jax.sharding import Mesh
from jax.sharding import PartitionSpec as P

STEP = 100
beta_first = 0.9
beta_second = 0.999
epsilon = 1e-08

DEVICE = pl.DeviceIdType.MESH
SIZES = {"y": 8, "z": 8, "x": 4, "c": 2}
TOKENS, FEATURES, OUTS, RANK = 512, 1024, 1024, 1024
CHUNKS = 4
WIDE = RANK // CHUNKS
HALF = TOKENS // 2
SHARE = TOKENS // 8
OWNED = 16

STAGE_AT = (0.0, 1.3, 4.0, 6.8, 8.2, 13.0, 17.5, 21.0)
STAGE_GAP = (0.1, 1.0, 1.0, 1.4, 1.8, 3.0, 3.0, 3.0)


def f32(value):
    return value.astype(jnp.float32)


def bf16(value):
    return value.astype(jnp.bfloat16)


def kernel(
    a_hbm, g_hbm, b_hbm, m1_hbm, m2_hbm,
    first_out, second_out, update_out,
    a_v, g_v, b_v, m1_v, m2_v, gt_v,
    p_v, r0_v, q_v, r1_v, t_v, r_v, s0_v, s_v, u_v, n_v, full_v,
    load_sem, pair_s, pair_r, rs_s, rs_r, ag_s, ag_r, join_s, join_r,
    one_s, one_r, two_s, two_r, norm_s, norm_r,
):
    at = {axis: lax.axis_index(axis) for axis in SIZES}
    x, c = at["x"], at["c"]

    def shifted(axis, offset):
        return lax.rem(at[axis] + offset, SIZES[axis])

    def columns(k):
        return pl.ds(k * WIDE, WIDE)

    def load(src, dst, index):
        copy = pltpu.make_async_copy(src, dst, load_sem.at[index])
        copy.start()
        return copy

    load_a = load(a_hbm, a_v, 0)
    load_b = [load(b_hbm.at[:, columns(k)], b_v.at[:, columns(k)], 1 + k) for k in range(CHUNKS)]
    load_g = load(g_hbm, g_v, 1 + CHUNKS)
    load_m1 = load(m1_hbm, m1_v, 2 + CHUNKS)
    load_m2 = load(m2_hbm, m2_v, 3 + CHUNKS)

    mp_peers = [
        {"x": shifted("x", dx), "c": shifted("c", dc)} for dx in range(4) for dc in range(2) if dx or dc
    ]
    barrier = pltpu.get_barrier_semaphore()
    peers = mp_peers + [{axis: shifted(axis, o)} for axis in ("y", "z") for o in range(1, 8)]
    for peer in peers:
        pl.semaphore_signal(barrier, inc=1, device_id=peer, device_id_type=DEVICE)

    sent = []
    coming = {}

    def send(src, dst, sems, slot, peer, tag):
        copy = pltpu.make_async_remote_copy(
            src_ref=src, dst_ref=dst, send_sem=sems[0].at[slot], recv_sem=sems[1].at[slot],
            device_id=peer, device_id_type=DEVICE,
        )
        copy.start()
        sent.append(copy)
        coming.setdefault(tag, []).append(copy)

    def arrive(tag):
        for copy in coming[tag]:
            copy.wait_recv()

    def axes_of(k):
        return ("y", "z") if k % 2 == 0 else ("z", "y")

    def project(k):
        load_b[k].wait()
        p_v[k] = bf16(jnp.dot(a_v[...], b_v[:, columns(k)], preferred_element_type=jnp.float32))
        if k == 0:
            pl.semaphore_wait(barrier, len(peers))
        send(
            p_v.at[k, pl.ds(pl.multiple_of((1 - c) * HALF, HALF), HALF)], r0_v.at[k],
            (pair_s, pair_r), k, {"c": 1 - c}, (0, k),
        )

    def pair_sum(k):
        arrive((0, k))
        mine = p_v[k, pl.ds(pl.multiple_of(c * HALF, HALF), HALF)]
        q_v[k] = bf16(f32(mine) + f32(r0_v[k]))
        for o in (2, 1, 3):
            to = shifted("x", o)
            send(
                q_v.at[k, pl.ds(pl.multiple_of(to * SHARE, SHARE), SHARE)], r1_v.at[k, o - 1],
                (rs_s, rs_r), 3 * k + o - 1, {"x": to}, (1, k),
            )

    def own_rows():
        return pl.ds(pl.multiple_of(c * HALF + x * SHARE, SHARE), SHARE)

    def token_share(k):
        arrive((1, k))
        total = f32(q_v[k, pl.ds(pl.multiple_of(x * SHARE, SHARE), SHARE)])
        for o in range(3):
            total = total + f32(r1_v[k, o])
        t_v[k, own_rows()] = bf16(total)
        for o in (2, 1, 3):
            send(
                t_v.at[k, own_rows()], t_v.at[k, own_rows()],
                (ag_s, ag_r), 3 * k + o - 1, {"x": shifted("x", o)}, (2, k),
            )

    def join(k):
        arrive((2, k))
        rows = pl.ds(pl.multiple_of(c * HALF, HALF), HALF)
        send(t_v.at[k, rows], t_v.at[k, rows], (join_s, join_r), k, {"c": 1 - c}, (3, k))

    def gradient(k):
        arrive((3, k))
        total = bf16(jnp.dot(gt_v[...], t_v[k], preferred_element_type=jnp.float32))
        if k % 2 == 0:
            r_v[k] = total.reshape(8, 128, WIDE)
        else:
            for y in range(8):
                r_v[k, :, pl.ds(16 * y, 16)] = total[128 * y : 128 * y + 128].reshape(8, 16, WIDE)
        axis = axes_of(k)[0]
        for o in (4, 3, 5, 2, 6, 1, 7):
            to = shifted(axis, o)
            send(r_v.at[k, to], s0_v.at[k, o - 1], (one_s, one_r), 7 * k + o - 1, {axis: to}, (4, k))

    def first_sum(k):
        arrive((4, k))
        total = f32(r_v[k, at[axes_of(k)[0]]])
        for o in range(7):
            total = total + f32(s0_v[k, o])
        s_v[k] = bf16(total).reshape(8, OWNED, WIDE)
        axis = axes_of(k)[1]
        for o in (4, 3, 5, 2, 6, 1, 7):
            to = shifted(axis, o)
            send(s_v.at[k, to], u_v.at[k, o - 1], (two_s, two_r), 7 * k + o - 1, {axis: to}, (5, k))

    def moments(k):
        arrive((5, k))
        reduced = f32(s_v[k, at[axes_of(k)[1]]])
        for o in range(7):
            reduced = reduced + f32(u_v[k, o])
        new_first = beta_first * m1_v[:, columns(k)] + (1.0 - beta_first) * reduced
        new_second = beta_second * m2_v[:, columns(k)] + (1.0 - beta_second) * reduced * reduced
        first_out[:, columns(k)] = new_first
        second_out[:, columns(k)] = new_second
        bias_first = 1.0 - beta_first**STEP
        bias_second = 1.0 - beta_second**STEP
        normed = new_first / bias_first / (jnp.sqrt(new_second / bias_second) + epsilon)
        me = 2 * x + c
        n_v[k, me] = bf16(normed)
        for i, peer in enumerate(mp_peers):
            send(n_v.at[k, me], n_v.at[k, me], (norm_s, norm_r), 7 * k + i, peer, (6, k))

    def expand(k):
        arrive((6, k))
        stacked = n_v[k].reshape(8 * OWNED, WIDE)
        part = lax.dot_general(
            stacked, b_v[:, columns(k)], (((1,), (1,)), ((), ())), preferred_element_type=jnp.float32
        )
        if k == 0:
            full_v[...] = part
        elif k < CHUNKS - 1:
            full_v[...] += part
        else:
            update_out[...] = bf16(full_v[...] + part).reshape(8, OWNED, FEATURES)

    stages = (project, pair_sum, token_share, join, gradient, first_sum, moments, expand)
    plan = sorted(
        (STAGE_AT[s] + k * STAGE_GAP[s], s, k) for s in range(len(stages)) for k in range(CHUNKS)
    )
    load_a.wait()
    turned = False
    for _, s, k in plan:
        if s == 1 and not turned:
            load_g.wait()
            gt_v[...] = g_v[...].T
            load_m1.wait()
            load_m2.wait()
            turned = True
        stages[s](k)
    for copy in sent:
        copy.wait_send()


def on_device(activations, out_grads, basis, moment1, moment2):
    def vmem(*shape, dtype=jnp.bfloat16):
        return pltpu.VMEM(shape, dtype)

    sems = pltpu.SemaphoreType.DMA
    n = CHUNKS
    pairs = [sems((count * n,)) for count in (1, 3, 3, 1, 7, 7, 7) for _ in range(2)]
    anywhere = pl.BlockSpec(memory_space=pl.ANY)
    in_vmem = pl.BlockSpec(memory_space=pltpu.VMEM)
    return pl.pallas_call(
        kernel,
        out_shape=(
            jax.ShapeDtypeStruct((OWNED, RANK), jnp.float32),
            jax.ShapeDtypeStruct((OWNED, RANK), jnp.float32),
            jax.ShapeDtypeStruct((8, OWNED, FEATURES), jnp.bfloat16),
        ),
        in_specs=[anywhere] * 5,
        out_specs=(in_vmem,) * 3,
        scratch_shapes=[
            vmem(TOKENS, FEATURES),
            vmem(TOKENS, OUTS),
            vmem(FEATURES, RANK),
            vmem(OWNED, RANK, dtype=jnp.float32),
            vmem(OWNED, RANK, dtype=jnp.float32),
            vmem(OUTS, TOKENS),
            vmem(n, TOKENS, WIDE),
            vmem(n, HALF, WIDE),
            vmem(n, HALF, WIDE),
            vmem(n, 3, SHARE, WIDE),
            vmem(n, TOKENS, WIDE),
            vmem(n, 8, 128, WIDE),
            vmem(n, 7, 128, WIDE),
            vmem(n, 8, OWNED, WIDE),
            vmem(n, 7, OWNED, WIDE),
            vmem(n, 8, OWNED, WIDE),
            vmem(8 * OWNED, FEATURES, dtype=jnp.float32),
            sems((4 + n,)),
        ]
        + pairs,
        compiler_params=pltpu.CompilerParams(
            collective_id=0, has_side_effects=True, vmem_limit_bytes=40 * 1024 * 1024
        ),
        name="projected_adam",
    )(activations, out_grads, basis, moment1, moment2)


def solution(mesh):
    finer = Mesh(mesh.devices.reshape(8, 8, 4, 2), ("y", "z", "x", "c"))
    dp, mp, owners = ("y", "z"), ("x", "c"), ("x", "c", "y", "z")
    in_specs = (P(dp, mp), P(dp, mp), P(mp, None), P(owners, None), P(owners, None))
    out_specs = (P(owners, None), P(owners, None), P(None, dp, mp))
    return jax.shard_map(
        on_device, mesh=finer, in_specs=in_specs, out_specs=out_specs, check_vma=False
    )
```

```python
import jax
import jax.numpy as jnp
from jax import lax
from jax.experimental import pallas as pl
from jax.experimental.pallas import tpu as pltpu
from jax.sharding import Mesh
from jax.sharding import PartitionSpec as P

STEP = 100
beta_first = 0.9
beta_second = 0.999
epsilon = 1e-08

DEVICE = pl.DeviceIdType.MESH
SIZES = {"y": 8, "z": 8, "x": 4, "c": 2}
TOKENS, FEATURES, OUTS, RANK = 512, 1024, 1024, 1024
CHUNKS = 2
SPLIT = 2
WIDE = RANK // CHUNKS
PART = WIDE // SPLIT
PARTS = CHUNKS * SPLIT
HALF = TOKENS // 2
SHARE = TOKENS // 8
OWNED = 16

STAGE_AT = (0.0, 2.2, 7.5, 13.0, 15.5, 21.0, 28.0, 33.0, 37.0)
STAGE_GAP = (1.4, 1.6, 2.8, 2.8, 2.8, 3.0, 3.0, 3.0, 3.0)


def f32(value):
    return value.astype(jnp.float32)


def bf16(value):
    return value.astype(jnp.bfloat16)


def kernel(
    a_hbm, g_hbm, b_hbm, m1_hbm, m2_hbm,
    first_out, second_out, update_out,
    a_v, g_v, b_v, m1_v, m2_v, gt_v,
    p_v, p32_v, r0_v, q_v, q32_v, r1_v, t_v, r_v, r32_v, hop_v, in_v, end_v,
    s_v, s32_v, u_v, n_v, full_v,
    load_sem, send_sem, pair_r, rs_r, ag_r, join_r, in_r, end_r, two_r, norm_r,
):
    at = {axis: lax.axis_index(axis) for axis in SIZES}
    x, c = at["x"], at["c"]

    def shifted(axis, offset):
        return lax.rem(at[axis] + offset + SIZES[axis], SIZES[axis])

    def columns(k):
        return pl.ds(k * WIDE, WIDE)

    def load(src, dst, index):
        copy = pltpu.make_async_copy(src, dst, load_sem.at[index])
        copy.start()
        return copy

    load_a = load(a_hbm, a_v, 0)
    load_b = [load(b_hbm.at[:, columns(k)], b_v.at[:, columns(k)], 1 + k) for k in range(CHUNKS)]
    load_g = load(g_hbm, g_v, 1 + CHUNKS)
    load_m1 = load(m1_hbm, m1_v, 2 + CHUNKS)
    load_m2 = load(m2_hbm, m2_v, 3 + CHUNKS)

    mp_peers = [
        {"x": shifted("x", dx), "c": shifted("c", dc)} for dx in range(4) for dc in range(2) if dx or dc
    ]
    barrier = pltpu.get_barrier_semaphore()
    peers = mp_peers + [{axis: shifted(axis, o)} for axis in ("y", "z") for o in range(1, 8)]
    for peer in peers:
        pl.semaphore_signal(barrier, inc=1, device_id=peer, device_id_type=DEVICE)

    def send(src, dst, kind, arrived, peer):
        pltpu.make_async_remote_copy(
            src_ref=src, dst_ref=dst, send_sem=send_sem.at[kind], recv_sem=arrived,
            device_id=peer, device_id_type=DEVICE,
        ).start()

    def await_bytes(ref, sem):
        pltpu.make_async_copy(ref, ref, sem).wait()

    def half(i):
        return pl.ds(pl.multiple_of(i * HALF, HALF), HALF)

    def share(i):
        return pl.ds(pl.multiple_of(i * SHARE, SHARE), SHARE)

    def project(k):
        load_b[k].wait()
        part = jnp.dot(a_v[...], b_v[:, columns(k)], preferred_element_type=jnp.float32)
        p_v[k] = bf16(part)
        p32_v[k] = part
        if k == 0:
            pl.semaphore_wait(barrier, len(peers))
        send(p_v.at[k, half(1 - c)], r0_v.at[k], 0, pair_r.at[k], {"c": 1 - c})

    def pair_sum(k):
        await_bytes(r0_v.at[k], pair_r.at[k])
        total = p32_v[k, half(c)] + f32(r0_v[k])
        q_v[k] = bf16(total)
        q32_v[k] = total
        for o in (2, 1, 3):
            to = shifted("x", o)
            send(q_v.at[k, share(to)], r1_v.at[k, o - 1], 1, rs_r.at[k], {"x": to})

    own_rows = share(4 * c + x)

    def token_share(k):
        await_bytes(r1_v.at[k], rs_r.at[k])
        total = q32_v[k, share(x)]
        for o in range(3):
            total = total + f32(r1_v[k, o])
        t_v[k, own_rows] = bf16(total)
        for o in (2, 1, 3):
            rows = t_v.at[k, own_rows]
            send(rows, rows, 2, ag_r.at[k], {"x": shifted("x", o)})

    def join(k):
        await_bytes(r1_v.at[k], ag_r.at[k])
        send(t_v.at[k, half(c)], t_v.at[k, half(c)], 3, join_r.at[k], {"c": 1 - c})

    def parts_of(k):
        return range(SPLIT * k, SPLIT * (k + 1))

    def route(j):
        axes = ("y", "z") if j % 2 == 0 else ("z", "y")
        return axes + ((1, -1) if (j // 2) % 2 == 0 else (-1, 1))

    def gradient(k):
        await_bytes(t_v.at[k, half(c)], join_r.at[k])
        total = jnp.dot(gt_v[...], t_v[k], preferred_element_type=jnp.float32)
        for i, j in enumerate(parts_of(k)):
            axis, _, far, _ = route(j)
            piece = total[:, PART * i : PART * (i + 1)]
            if axis == "y":
                r32_v[j] = piece.reshape(8, 128, PART)
                r_v[j] = bf16(piece).reshape(8, 128, PART)
            else:
                for y in range(8):
                    rows = piece[128 * y : 128 * y + 128].reshape(8, 16, PART)
                    r32_v[j, :, pl.ds(16 * y, 16)] = rows
                    r_v[j, :, pl.ds(16 * y, 16)] = bf16(rows)
        for j in parts_of(k):
            axis, _, far, near = route(j)
            send(r_v.at[j, shifted(axis, 4)], in_v.at[j, 2], 4, in_r.at[j], {axis: shifted(axis, 2 * far)})
            for i, d in enumerate((far, near)):
                to = {axis: shifted(axis, d)}
                send(r_v.at[j, shifted(axis, 3 * d)], in_v.at[j, i], 4, in_r.at[j], to)
        for j in parts_of(k):
            axis, _, far, near = route(j)
            for i, d in enumerate((far, near)):
                to = shifted(axis, d)
                send(r_v.at[j, to], end_v.at[j, i], 4, end_r.at[j], {axis: to})

    def jump(k):
        for j in parts_of(k):
            await_bytes(in_v.at[j], in_r.at[j])
            axis, _, far, near = route(j)
            for i, d in enumerate((far, near)):
                to = shifted(axis, 2 * d)
                total = r32_v[j, to] + f32(in_v[j, i])
                if d == far:
                    total = total + f32(in_v[j, 2])
                hop_v[j, i] = bf16(total)
                send(hop_v.at[j, i], end_v.at[j, 2 + i], 5, end_r.at[j], {axis: to})

    def first_sum(k):
        for j in parts_of(k):
            await_bytes(end_v.at[j], end_r.at[j])
            axis, axis2, _, _ = route(j)
            total = r32_v[j, at[axis]]
            for i in range(4):
                total = total + f32(end_v[j, i])
            total = total.reshape(8, OWNED, PART)
            s_v[j] = bf16(total)
            s32_v[j] = total
            for o in (4, 3, 5, 2, 6, 1, 7):
                to = shifted(axis2, o)
                send(s_v.at[j, to], u_v.at[j, o - 1], 6, two_r.at[j], {axis2: to})

    def moments(k):
        me = 2 * x + c
        for i, j in enumerate(parts_of(k)):
            await_bytes(u_v.at[j], two_r.at[j])
            cols = pl.ds(j * PART, PART)
            reduced = s32_v[j, at[route(j)[1]]]
            for o in range(7):
                reduced = reduced + f32(u_v[j, o])
            new_first = beta_first * m1_v[:, cols] + (1.0 - beta_first) * reduced
            new_second = beta_second * m2_v[:, cols] + (1.0 - beta_second) * reduced * reduced
            first_out[:, cols] = new_first
            second_out[:, cols] = new_second
            bias_first = 1.0 - beta_first**STEP
            bias_second = 1.0 - beta_second**STEP
            normed = new_first / bias_first / (jnp.sqrt(new_second / bias_second) + epsilon)
            n_v[k, me, :, pl.ds(i * PART, PART)] = bf16(normed)
        for peer in mp_peers:
            send(n_v.at[k, me], n_v.at[k, me], 7, norm_r.at[k], peer)

    def expand(k):
        await_bytes(n_v.at[k, pl.ds(0, 7)], norm_r.at[k])
        stacked = n_v[k].reshape(8 * OWNED, WIDE)
        part = lax.dot_general(
            stacked, b_v[:, columns(k)], (((1,), (1,)), ((), ())), preferred_element_type=jnp.float32
        )
        if k == 0:
            full_v[...] = part
        elif k < CHUNKS - 1:
            full_v[...] += part
        else:
            update_out[...] = bf16(full_v[...] + part).reshape(8, OWNED, FEATURES)

    stages = (project, pair_sum, token_share, join, gradient, jump, first_sum, moments, expand)
    plan = sorted(
        (STAGE_AT[s] + k * STAGE_GAP[s], s, k) for s in range(len(stages)) for k in range(CHUNKS)
    )
    load_a.wait()
    turned = False
    for _, s, k in plan:
        if s == 2 and not turned:
            load_g.wait()
            gt_v[...] = g_v[...].T
            load_m1.wait()
            load_m2.wait()
            turned = True
        stages[s](k)
    gone = (
        r0_v, r1_v, r1_v, r0_v, r_v.at[:, pl.ds(0, 5)], hop_v, u_v, n_v.at[:, pl.ds(0, 7)],
    )
    for kind, ref in enumerate(gone):
        await_bytes(ref, send_sem.at[kind])


def write_out(first_v, second_v, update_v, first_hbm, second_hbm, update_hbm, sem):
    pairs = ((update_v, update_hbm), (first_v, first_hbm), (second_v, second_hbm))
    copies = [pltpu.make_async_copy(src, dst, sem.at[i]) for i, (src, dst) in enumerate(pairs)]
    for copy in copies:
        copy.start()
    for copy in copies:
        copy.wait()


def on_device(activations, out_grads, basis, moment1, moment2):
    def vmem(*shape, dtype=jnp.bfloat16):
        return pltpu.VMEM(shape, dtype)

    wide = jnp.float32
    sems = pltpu.SemaphoreType.DMA
    n, m = CHUNKS, PARTS
    counts = (4 + n, 8, n, n, n, n, m, m, m, n)
    in_hbm = pl.BlockSpec(memory_space=pltpu.HBM)
    in_vmem = pl.BlockSpec(memory_space=pltpu.VMEM)
    out_shape = (
        jax.ShapeDtypeStruct((OWNED, RANK), jnp.float32),
        jax.ShapeDtypeStruct((OWNED, RANK), jnp.float32),
        jax.ShapeDtypeStruct((8, OWNED, FEATURES), jnp.bfloat16),
    )
    results = pl.pallas_call(
        kernel,
        out_shape=out_shape,
        in_specs=[in_hbm] * 5,
        out_specs=(in_vmem,) * 3,
        scratch_shapes=[
            vmem(TOKENS, FEATURES),
            vmem(TOKENS, OUTS),
            vmem(FEATURES, RANK),
            vmem(OWNED, RANK, dtype=wide),
            vmem(OWNED, RANK, dtype=wide),
            vmem(OUTS, TOKENS),
            vmem(n, TOKENS, WIDE),
            vmem(n, TOKENS, WIDE, dtype=wide),
            vmem(n, HALF, WIDE),
            vmem(n, HALF, WIDE),
            vmem(n, HALF, WIDE, dtype=wide),
            vmem(n, 3, SHARE, WIDE),
            vmem(n, TOKENS, WIDE),
            vmem(m, 8, 128, PART),
            vmem(m, 8, 128, PART, dtype=wide),
            vmem(m, 2, 128, PART),
            vmem(m, 3, 128, PART),
            vmem(m, 4, 128, PART),
            vmem(m, 8, OWNED, PART),
            vmem(m, 8, OWNED, PART, dtype=wide),
            vmem(m, 7, OWNED, PART),
            vmem(n, 8, OWNED, WIDE),
            vmem(8 * OWNED, FEATURES, dtype=wide),
        ]
        + [sems((count,)) for count in counts],
        compiler_params=pltpu.CompilerParams(
            collective_id=0, has_side_effects=True, vmem_limit_bytes=55060 * 1024
        ),
        name="projected_adam",
    )(activations, out_grads, basis, moment1, moment2)
    return pl.pallas_call(
        write_out,
        out_shape=out_shape,
        in_specs=[in_vmem] * 3,
        out_specs=(in_hbm,) * 3,
        scratch_shapes=[sems((3,))],
        compiler_params=pltpu.CompilerParams(vmem_limit_bytes=1024 * 1024),
        name="write_out",
    )(*results)


def solution(mesh):
    finer = Mesh(mesh.devices.reshape(8, 8, 4, 2), ("y", "z", "x", "c"))
    dp, mp, owners = ("y", "z"), ("x", "c"), ("x", "c", "y", "z")
    in_specs = (P(dp, mp), P(dp, mp), P(mp, None), P(owners, None), P(owners, None))
    out_specs = (P(owners, None), P(owners, None), P(None, dp, mp))
    return jax.shard_map(
        on_device, mesh=finer, in_specs=in_specs, out_specs=out_specs, check_vma=False
    )
```

```python
import jax
import jax.numpy as jnp
from jax import lax
from jax.experimental import pallas as pl
from jax.experimental.pallas import tpu as pltpu
from jax.sharding import Mesh
from jax.sharding import PartitionSpec as P

STEP = 100
beta_first = 0.9
beta_second = 0.999
epsilon = 1e-08

DEVICE = pl.DeviceIdType.MESH
SIZES = {"y": 8, "z": 8, "x": 4, "c": 2}
TOKENS, FEATURES, OUTS, RANK = 512, 1024, 1024, 1024
CHUNKS = 2
SPLIT = 2
WIDE = RANK // CHUNKS
PART = WIDE // SPLIT
PARTS = CHUNKS * SPLIT
HALF = TOKENS // 2
SHARE = TOKENS // 8
OWNED = 16

ORDER = (
    (0, 0), (0, 1), (1, 0), (1, 1), (2, 0), (2, 1), (3, 0), (4, 0), (3, 1),
    (4, 1), (5, 0), (5, 1), (6, 0), (6, 1), (7, 0), (7, 1), (8, 0), (8, 1),
)


def f32(value):
    return value.astype(jnp.float32)


def bf16(value):
    return value.astype(jnp.bfloat16)


def kernel(
    a_hbm, g_hbm, b_hbm, m1_hbm, m2_hbm,
    first_out, second_out, up0, up1, up2, up3,
    a_v, g_v, b_v, m1_v, m2_v, gt_v,
    p_v, p32_v, r0_v, q_v, q32_v, r1_v, t_v, r_v, r32_v, hop_v, in_v, end_v,
    s_v, s32_v, u_v, n_v, full_v,
    load_sem, send_sem, pair_r, rs_r, ag_r, join_r, in_r, end_r, two_r, norm_r,
):
    at = {axis: lax.axis_index(axis) for axis in SIZES}
    x, c = at["x"], at["c"]

    def shifted(axis, offset):
        return lax.rem(at[axis] + offset + SIZES[axis], SIZES[axis])

    def columns(k):
        return pl.ds(k * WIDE, WIDE)

    def load(src, dst, index):
        copy = pltpu.make_async_copy(src, dst, load_sem.at[index])
        copy.start()
        return copy

    load_a = load(a_hbm, a_v, 0)
    load_b = [load(b_hbm.at[:, columns(k)], b_v.at[:, columns(k)], 1 + k) for k in range(CHUNKS)]
    load_g = load(g_hbm, g_v, 1 + CHUNKS)
    load_m1 = load(m1_hbm, m1_v, 2 + CHUNKS)
    load_m2 = load(m2_hbm, m2_v, 3 + CHUNKS)

    mp_peers = [
        {"x": shifted("x", dx), "c": shifted("c", dc)} for dx in range(4) for dc in range(2) if dx or dc
    ]
    barrier = pltpu.get_barrier_semaphore()
    peers = mp_peers + [{axis: shifted(axis, o)} for axis in ("y", "z") for o in range(1, 8)]
    for peer in peers:
        pl.semaphore_signal(barrier, inc=1, device_id=peer, device_id_type=DEVICE)

    def send(src, dst, kind, arrived, peer):
        pltpu.make_async_remote_copy(
            src_ref=src, dst_ref=dst, send_sem=send_sem.at[kind], recv_sem=arrived,
            device_id=peer, device_id_type=DEVICE,
        ).start()

    def await_bytes(ref, sem):
        pltpu.make_async_copy(ref, ref, sem).wait()

    def half(i):
        return pl.ds(pl.multiple_of(i * HALF, HALF), HALF)

    def share(i):
        return pl.ds(pl.multiple_of(i * SHARE, SHARE), SHARE)

    def project(k):
        load_b[k].wait()
        part = jnp.dot(a_v[...], b_v[:, columns(k)], preferred_element_type=jnp.float32)
        p_v[k] = bf16(part)
        p32_v[k] = part
        if k == 0:
            pl.semaphore_wait(barrier, len(peers))
        send(p_v.at[k, half(1 - c)], r0_v.at[k], 0, pair_r.at[k], {"c": 1 - c})

    def pair_sum(k):
        await_bytes(r0_v.at[k], pair_r.at[k])
        total = p32_v[k, half(c)] + f32(r0_v[k])
        q_v[k] = bf16(total)
        q32_v[k] = total
        for o in (2, 1, 3):
            to = shifted("x", o)
            send(q_v.at[k, share(to)], r1_v.at[k, o - 1], 1, rs_r.at[k], {"x": to})

    own_rows = share(4 * c + x)

    def token_share(k):
        await_bytes(r1_v.at[k], rs_r.at[k])
        total = q32_v[k, share(x)]
        for o in range(3):
            total = total + f32(r1_v[k, o])
        t_v[k, own_rows] = bf16(total)
        for o in (2, 1, 3):
            rows = t_v.at[k, own_rows]
            send(rows, rows, 2, ag_r.at[k], {"x": shifted("x", o)})

    def join(k):
        await_bytes(r1_v.at[k], ag_r.at[k])
        send(t_v.at[k, half(c)], t_v.at[k, half(c)], 3, join_r.at[k], {"c": 1 - c})

    def parts_of(k):
        return range(SPLIT * k, SPLIT * (k + 1))

    def route(j):
        axes = ("y", "z") if j % 2 == 0 else ("z", "y")
        return axes + ((1, -1) if (j // 2) % 2 == 0 else (-1, 1))

    def gradient(k):
        await_bytes(t_v.at[k, half(c)], join_r.at[k])
        total = jnp.dot(gt_v[...], t_v[k], preferred_element_type=jnp.float32)
        for i, j in enumerate(parts_of(k)):
            axis, _, far, _ = route(j)
            piece = total[:, PART * i : PART * (i + 1)]
            if axis == "y":
                r32_v[j] = piece.reshape(8, 128, PART)
                r_v[j] = bf16(piece).reshape(8, 128, PART)
            else:
                for y in range(8):
                    rows = piece[128 * y : 128 * y + 128].reshape(8, 16, PART)
                    r32_v[j, :, pl.ds(16 * y, 16)] = rows
                    r_v[j, :, pl.ds(16 * y, 16)] = bf16(rows)
        for j in parts_of(k):
            axis, _, far, near = route(j)
            send(r_v.at[j, shifted(axis, 4)], in_v.at[j, 2], 4, in_r.at[j], {axis: shifted(axis, 2 * far)})
            for i, d in enumerate((far, near)):
                to = {axis: shifted(axis, d)}
                send(r_v.at[j, shifted(axis, 3 * d)], in_v.at[j, i], 4, in_r.at[j], to)
        for j in parts_of(k):
            axis, _, far, near = route(j)
            for i, d in enumerate((far, near)):
                to = shifted(axis, d)
                send(r_v.at[j, to], end_v.at[j, i], 4, end_r.at[j], {axis: to})

    def jump(k):
        for j in parts_of(k):
            await_bytes(in_v.at[j], in_r.at[j])
            axis, _, far, near = route(j)
            for i, d in enumerate((far, near)):
                to = shifted(axis, 2 * d)
                total = r32_v[j, to] + f32(in_v[j, i])
                if d == far:
                    total = total + f32(in_v[j, 2])
                hop_v[j, i] = bf16(total)
                send(hop_v.at[j, i], end_v.at[j, 2 + i], 5, end_r.at[j], {axis: to})

    def first_sum(k):
        for j in parts_of(k):
            await_bytes(end_v.at[j], end_r.at[j])
            axis, axis2, _, _ = route(j)
            total = r32_v[j, at[axis]]
            for i in range(4):
                total = total + f32(end_v[j, i])
            total = total.reshape(8, OWNED, PART)
            s_v[j] = bf16(total)
            s32_v[j] = total
            for o in (4, 3, 5, 2, 6, 1, 7):
                to = shifted(axis2, o)
                send(s_v.at[j, to], u_v.at[j, o - 1], 6, two_r.at[j], {axis2: to})

    def moments(k):
        me = 2 * x + c
        for i, j in enumerate(parts_of(k)):
            await_bytes(u_v.at[j], two_r.at[j])
            cols = pl.ds(j * PART, PART)
            reduced = s32_v[j, at[route(j)[1]]]
            for o in range(7):
                reduced = reduced + f32(u_v[j, o])
            new_first = beta_first * m1_v[:, cols] + (1.0 - beta_first) * reduced
            new_second = beta_second * m2_v[:, cols] + (1.0 - beta_second) * reduced * reduced
            first_out[:, cols] = new_first
            second_out[:, cols] = new_second
            bias_first = 1.0 - beta_first**STEP
            bias_second = 1.0 - beta_second**STEP
            normed = new_first / bias_first / (jnp.sqrt(new_second / bias_second) + epsilon)
            n_v[k, me, :, pl.ds(i * PART, PART)] = bf16(normed)
        for peer in mp_peers:
            send(n_v.at[k, me], n_v.at[k, me], 7, norm_r.at[k], peer)

    def expand(k):
        await_bytes(n_v.at[k, pl.ds(0, 7)], norm_r.at[k])
        stacked = n_v[k].reshape(8 * OWNED, WIDE)
        part = lax.dot_general(
            stacked, b_v[:, columns(k)], (((1,), (1,)), ((), ())), preferred_element_type=jnp.float32
        )
        if k == 0:
            full_v[...] = part
        elif k < CHUNKS - 1:
            full_v[...] += part
        else:
            whole = bf16(full_v[...] + part).reshape(8, OWNED, FEATURES)
            for i, out in enumerate((up0, up1, up2, up3)):
                out[...] = whole[2 * i : 2 * i + 2]

    stages = (project, pair_sum, token_share, join, gradient, jump, first_sum, moments, expand)
    plan = [(0, s, k) for s, k in ORDER]
    load_a.wait()
    turned = False
    for _, s, k in plan:
        if s == 2 and not turned:
            load_g.wait()
            gt_v[...] = g_v[...].T
            load_m1.wait()
            load_m2.wait()
            turned = True
        stages[s](k)
    gone = (
        r0_v, r1_v, r1_v, r0_v, r_v.at[:, pl.ds(0, 5)], hop_v, u_v, n_v.at[:, pl.ds(0, 7)],
    )
    for kind, ref in enumerate(gone):
        await_bytes(ref, send_sem.at[kind])


def write_out(first_v, second_v, *rest):
    pieces, (first_hbm, second_hbm, update_hbm, sem) = rest[:4], rest[4:]
    pairs = [(piece, update_hbm.at[pl.ds(2 * i, 2)]) for i, piece in enumerate(pieces)]
    pairs += [(first_v, first_hbm), (second_v, second_hbm)]
    copies = [pltpu.make_async_copy(src, dst, sem.at[i]) for i, (src, dst) in enumerate(pairs)]
    for copy in copies:
        copy.start()
    for copy in copies:
        copy.wait()


def on_device(activations, out_grads, basis, moment1, moment2):
    def vmem(*shape, dtype=jnp.bfloat16):
        return pltpu.VMEM(shape, dtype)

    wide = jnp.float32
    sems = pltpu.SemaphoreType.DMA
    n, m = CHUNKS, PARTS
    counts = (4 + n, 8, n, n, n, n, m, m, m, n)
    in_hbm = pl.BlockSpec(memory_space=pltpu.HBM)
    in_vmem = pl.BlockSpec(memory_space=pltpu.VMEM)
    out_shape = (
        jax.ShapeDtypeStruct((OWNED, RANK), jnp.float32),
        jax.ShapeDtypeStruct((OWNED, RANK), jnp.float32),
        jax.ShapeDtypeStruct((8, OWNED, FEATURES), jnp.bfloat16),
    )
    results = pl.pallas_call(
        kernel,
        out_shape=out_shape[:2] + (jax.ShapeDtypeStruct((2, OWNED, FEATURES), jnp.bfloat16),) * 4,
        in_specs=[in_hbm] * 5,
        out_specs=(in_vmem,) * 6,
        scratch_shapes=[
            vmem(TOKENS, FEATURES),
            vmem(TOKENS, OUTS),
            vmem(FEATURES, RANK),
            vmem(OWNED, RANK, dtype=wide),
            vmem(OWNED, RANK, dtype=wide),
            vmem(OUTS, TOKENS),
            vmem(n, TOKENS, WIDE),
            vmem(n, TOKENS, WIDE, dtype=wide),
            vmem(n, HALF, WIDE),
            vmem(n, HALF, WIDE),
            vmem(n, HALF, WIDE, dtype=wide),
            vmem(n, 3, SHARE, WIDE),
            vmem(n, TOKENS, WIDE),
            vmem(m, 8, 128, PART),
            vmem(m, 8, 128, PART, dtype=wide),
            vmem(m, 2, 128, PART),
            vmem(m, 3, 128, PART),
            vmem(m, 4, 128, PART),
            vmem(m, 8, OWNED, PART),
            vmem(m, 8, OWNED, PART, dtype=wide),
            vmem(m, 7, OWNED, PART),
            vmem(n, 8, OWNED, WIDE),
            vmem(8 * OWNED, FEATURES, dtype=wide),
        ]
        + [sems((count,)) for count in counts],
        compiler_params=pltpu.CompilerParams(
            collective_id=0, has_side_effects=True, vmem_limit_bytes=54800 * 1024
        ),
        name="projected_adam",
    )(activations, out_grads, basis, moment1, moment2)
    return pl.pallas_call(
        write_out,
        out_shape=out_shape,
        in_specs=[in_vmem] * 6,
        out_specs=(in_hbm,) * 3,
        scratch_shapes=[sems((6,))],
        compiler_params=pltpu.CompilerParams(vmem_limit_bytes=1024 * 1024),
        name="write_out",
    )(*results)


def solution(mesh):
    finer = Mesh(mesh.devices.reshape(8, 8, 4, 2), ("y", "z", "x", "c"))
    dp, mp, owners = ("y", "z"), ("x", "c"), ("x", "c", "y", "z")
    in_specs = (P(dp, mp), P(dp, mp), P(mp, None), P(owners, None), P(owners, None))
    out_specs = (P(owners, None), P(owners, None), P(None, dp, mp))
    return jax.shard_map(
        on_device, mesh=finer, in_specs=in_specs, out_specs=out_specs, check_vma=False
    )
```

```python
import jax
import jax.numpy as jnp
from jax import lax
from jax.experimental import pallas as pl
from jax.experimental.pallas import tpu as pltpu
from jax.sharding import Mesh
from jax.sharding import PartitionSpec as P

STEP = 100
beta_first = 0.9
beta_second = 0.999
epsilon = 1e-08

DEVICE = pl.DeviceIdType.MESH
SIZES = {"y": 8, "z": 8, "x": 4, "c": 2}
TOKENS, FEATURES, OUTS, RANK = 512, 1024, 1024, 1024
CHUNKS = 2
SPLIT = 2
WIDE = RANK // CHUNKS
PART = WIDE // SPLIT
PARTS = CHUNKS * SPLIT
HALF = TOKENS // 2
SHARE = TOKENS // 8
OWNED = 16

ORDER = (
    (0, 0), (0, 1), (1, 0), (1, 1), (2, 0), (2, 1), (3, 0), (4, 0), (3, 1),
    (4, 1), (5, 0), (5, 1), (6, 0), (6, 1), (7, 0), (7, 1), (8, 0), (8, 1),
)


def f32(value):
    return value.astype(jnp.float32)


def bf16(value):
    return value.astype(jnp.bfloat16)


def kernel(
    a_hbm, g_hbm, b_hbm, m1_hbm, m2_hbm,
    first_out, second_out, up0, up1, up2, up3,
    a_v, g_v, b_v, m1_v, m2_v, gt_v,
    p_v, p32_v, r0_v, q_v, q32_v, r1_v, t_v, r_v, r32_v, hop_v, in_v, end_v,
    s_v, s32_v, u_v, n_v, full_v,
    load_sem, send_sem, pair_r, rs_r, ag_r, join_r, in_r, end_r, two_r, norm_r,
):
    at = {axis: lax.axis_index(axis) for axis in SIZES}
    x, c = at["x"], at["c"]

    def shifted(axis, offset):
        return lax.rem(at[axis] + offset + SIZES[axis], SIZES[axis])

    def columns(k):
        return pl.ds(k * WIDE, WIDE)

    def load(src, dst, index):
        copy = pltpu.make_async_copy(src, dst, load_sem.at[index])
        copy.start()
        return copy

    load_a = load(a_hbm, a_v, 0)
    load_b = [load(b_hbm.at[:, columns(k)], b_v.at[:, columns(k)], 1 + k) for k in range(CHUNKS)]
    load_g = load(g_hbm, g_v, 1 + CHUNKS)
    load_m1 = load(m1_hbm, m1_v, 2 + CHUNKS)
    load_m2 = load(m2_hbm, m2_v, 3 + CHUNKS)

    mp_peers = [
        {"x": shifted("x", dx), "c": shifted("c", dc)} for dx in (1, 3, 2, 0) for dc in range(2) if dx or dc
    ]
    barrier = pltpu.get_barrier_semaphore()
    peers = mp_peers + [{axis: shifted(axis, o)} for axis in ("y", "z") for o in range(1, 8)]
    for peer in peers:
        pl.semaphore_signal(barrier, inc=1, device_id=peer, device_id_type=DEVICE)

    def send(src, dst, kind, arrived, peer):
        pltpu.make_async_remote_copy(
            src_ref=src, dst_ref=dst, send_sem=send_sem.at[kind], recv_sem=arrived,
            device_id=peer, device_id_type=DEVICE,
        ).start()

    def await_bytes(ref, sem):
        pltpu.make_async_copy(ref, ref, sem).wait()

    def half(i):
        return pl.ds(pl.multiple_of(i * HALF, HALF), HALF)

    def share(i):
        return pl.ds(pl.multiple_of(i * SHARE, SHARE), SHARE)

    def project(k):
        load_b[k].wait()
        part = jnp.dot(a_v[...], b_v[:, columns(k)], preferred_element_type=jnp.float32)
        p_v[k] = bf16(part)
        p32_v[k] = part
        if k == 0:
            pl.semaphore_wait(barrier, len(peers))
        send(p_v.at[k, half(1 - c)], r0_v.at[k], 0, pair_r.at[k], {"c": 1 - c})

    def pair_sum(k):
        await_bytes(r0_v.at[k], pair_r.at[k])
        total = p32_v[k, half(c)] + f32(r0_v[k])
        q_v[k] = bf16(total)
        q32_v[k] = total
        for o in (1, 3, 2):
            to = shifted("x", o)
            send(q_v.at[k, share(to)], r1_v.at[k, o - 1], 1, rs_r.at[k], {"x": to})

    own_rows = share(4 * c + x)

    def token_share(k):
        await_bytes(r1_v.at[k], rs_r.at[k])
        total = q32_v[k, share(x)]
        for o in range(3):
            total = total + f32(r1_v[k, o])
        t_v[k, own_rows] = bf16(total)
        for o in (1, 3, 2):
            rows = t_v.at[k, own_rows]
            send(rows, rows, 2, ag_r.at[k], {"x": shifted("x", o)})

    def join(k):
        await_bytes(r1_v.at[k], ag_r.at[k])
        send(t_v.at[k, half(c)], t_v.at[k, half(c)], 3, join_r.at[k], {"c": 1 - c})

    def parts_of(k):
        return range(SPLIT * k, SPLIT * (k + 1))

    def route(j):
        axes = ("y", "z") if j % 2 == 0 else ("z", "y")
        return axes + ((1, -1) if (j // 2) % 2 == 0 else (-1, 1))

    def gradient(k):
        await_bytes(t_v.at[k, half(c)], join_r.at[k])
        total = jnp.dot(gt_v[...], t_v[k], preferred_element_type=jnp.float32)
        for i, j in enumerate(parts_of(k)):
            axis, _, far, _ = route(j)
            piece = total[:, PART * i : PART * (i + 1)]
            if axis == "y":
                r32_v[j] = piece.reshape(8, 128, PART)
                r_v[j] = bf16(piece).reshape(8, 128, PART)
            else:
                for y in range(8):
                    rows = piece[128 * y : 128 * y + 128].reshape(8, 16, PART)
                    r32_v[j, :, pl.ds(16 * y, 16)] = rows
                    r_v[j, :, pl.ds(16 * y, 16)] = bf16(rows)
        for j in parts_of(k):
            axis, _, far, near = route(j)
            send(r_v.at[j, shifted(axis, 4)], in_v.at[j, 2], 4, in_r.at[j], {axis: shifted(axis, 2 * far)})
            for i, d in enumerate((far, near)):
                to = {axis: shifted(axis, d)}
                send(r_v.at[j, shifted(axis, 3 * d)], in_v.at[j, i], 4, in_r.at[j], to)
        for j in parts_of(k):
            axis, _, far, near = route(j)
            for i, d in enumerate((far, near)):
                to = shifted(axis, d)
                send(r_v.at[j, to], end_v.at[j, i], 4, end_r.at[j], {axis: to})

    def jump(k):
        for j in parts_of(k):
            await_bytes(in_v.at[j], in_r.at[j])
            axis, _, far, near = route(j)
            for i, d in enumerate((far, near)):
                to = shifted(axis, 2 * d)
                total = r32_v[j, to] + f32(in_v[j, i])
                if d == far:
                    total = total + f32(in_v[j, 2])
                hop_v[j, i] = bf16(total)
                send(hop_v.at[j, i], end_v.at[j, 2 + i], 5, end_r.at[j], {axis: to})

    def first_sum(k):
        for j in parts_of(k):
            await_bytes(end_v.at[j], end_r.at[j])
            axis, axis2, _, _ = route(j)
            total = r32_v[j, at[axis]]
            for i in range(4):
                total = total + f32(end_v[j, i])
            total = total.reshape(8, OWNED, PART)
            s_v[j] = bf16(total)
            s32_v[j] = total
            for o in (4, 3, 5, 2, 6, 1, 7):
                to = shifted(axis2, o)
                send(s_v.at[j, to], u_v.at[j, o - 1], 6, two_r.at[j], {axis2: to})

    def moments(k):
        me = 2 * x + c
        for i, j in enumerate(parts_of(k)):
            await_bytes(u_v.at[j], two_r.at[j])
            cols = pl.ds(j * PART, PART)
            reduced = s32_v[j, at[route(j)[1]]]
            for o in range(7):
                reduced = reduced + f32(u_v[j, o])
            new_first = beta_first * m1_v[:, cols] + (1.0 - beta_first) * reduced
            new_second = beta_second * m2_v[:, cols] + (1.0 - beta_second) * reduced * reduced
            first_out[:, cols] = new_first
            second_out[:, cols] = new_second
            bias_first = 1.0 - beta_first**STEP
            bias_second = 1.0 - beta_second**STEP
            normed = new_first / bias_first / (jnp.sqrt(new_second / bias_second) + epsilon)
            n_v[k, me, :, pl.ds(i * PART, PART)] = bf16(normed)
        for peer in mp_peers:
            send(n_v.at[k, me], n_v.at[k, me], 7, norm_r.at[k], peer)

    def expand(k):
        await_bytes(n_v.at[k, pl.ds(0, 7)], norm_r.at[k])
        stacked = n_v[k].reshape(8 * OWNED, WIDE)
        part = lax.dot_general(
            stacked, b_v[:, columns(k)], (((1,), (1,)), ((), ())), preferred_element_type=jnp.float32
        )
        if k == 0:
            full_v[...] = part
        elif k < CHUNKS - 1:
            full_v[...] += part
        else:
            whole = bf16(full_v[...] + part).reshape(8, OWNED, FEATURES)
            for i, out in enumerate((up0, up1, up2, up3)):
                out[...] = whole[2 * i : 2 * i + 2]

    stages = (project, pair_sum, token_share, join, gradient, jump, first_sum, moments, expand)
    plan = [(0, s, k) for s, k in ORDER]
    load_a.wait()
    turned = False
    for _, s, k in plan:
        if s == 2 and not turned:
            load_g.wait()
            gt_v[...] = g_v[...].T
            load_m1.wait()
            load_m2.wait()
            turned = True
        stages[s](k)
    gone = (
        r0_v, r1_v, r1_v, r0_v, r_v.at[:, pl.ds(0, 5)], hop_v, u_v, n_v.at[:, pl.ds(0, 7)],
    )
    for kind, ref in enumerate(gone):
        await_bytes(ref, send_sem.at[kind])


def write_out(first_v, second_v, *rest):
    pieces, (first_hbm, second_hbm, update_hbm, sem) = rest[:4], rest[4:]
    pairs = [(piece, update_hbm.at[pl.ds(2 * i, 2)]) for i, piece in enumerate(pieces)]
    pairs += [(first_v, first_hbm), (second_v, second_hbm)]
    copies = [pltpu.make_async_copy(src, dst, sem.at[i]) for i, (src, dst) in enumerate(pairs)]
    for copy in copies:
        copy.start()
    for copy in copies:
        copy.wait()


def on_device(activations, out_grads, basis, moment1, moment2):
    def vmem(*shape, dtype=jnp.bfloat16):
        return pltpu.VMEM(shape, dtype)

    wide = jnp.float32
    sems = pltpu.SemaphoreType.DMA
    n, m = CHUNKS, PARTS
    counts = (4 + n, 8, n, n, n, n, m, m, m, n)
    in_hbm = pl.BlockSpec(memory_space=pltpu.HBM)
    in_vmem = pl.BlockSpec(memory_space=pltpu.VMEM)
    out_shape = (
        jax.ShapeDtypeStruct((OWNED, RANK), jnp.float32),
        jax.ShapeDtypeStruct((OWNED, RANK), jnp.float32),
        jax.ShapeDtypeStruct((8, OWNED, FEATURES), jnp.bfloat16),
    )
    results = pl.pallas_call(
        kernel,
        out_shape=out_shape[:2] + (jax.ShapeDtypeStruct((2, OWNED, FEATURES), jnp.bfloat16),) * 4,
        in_specs=[in_hbm] * 5,
        out_specs=(in_vmem,) * 6,
        scratch_shapes=[
            vmem(TOKENS, FEATURES),
            vmem(TOKENS, OUTS),
            vmem(FEATURES, RANK),
            vmem(OWNED, RANK, dtype=wide),
            vmem(OWNED, RANK, dtype=wide),
            vmem(OUTS, TOKENS),
            vmem(n, TOKENS, WIDE),
            vmem(n, TOKENS, WIDE, dtype=wide),
            vmem(n, HALF, WIDE),
            vmem(n, HALF, WIDE),
            vmem(n, HALF, WIDE, dtype=wide),
            vmem(n, 3, SHARE, WIDE),
            vmem(n, TOKENS, WIDE),
            vmem(m, 8, 128, PART),
            vmem(m, 8, 128, PART, dtype=wide),
            vmem(m, 2, 128, PART),
            vmem(m, 3, 128, PART),
            vmem(m, 4, 128, PART),
            vmem(m, 8, OWNED, PART),
            vmem(m, 8, OWNED, PART, dtype=wide),
            vmem(m, 7, OWNED, PART),
            vmem(n, 8, OWNED, WIDE),
            vmem(8 * OWNED, FEATURES, dtype=wide),
        ]
        + [sems((count,)) for count in counts],
        compiler_params=pltpu.CompilerParams(
            collective_id=0, has_side_effects=True, vmem_limit_bytes=54800 * 1024
        ),
        name="projected_adam",
    )(activations, out_grads, basis, moment1, moment2)
    return pl.pallas_call(
        write_out,
        out_shape=out_shape,
        in_specs=[in_vmem] * 6,
        out_specs=(in_hbm,) * 3,
        scratch_shapes=[sems((6,))],
        compiler_params=pltpu.CompilerParams(vmem_limit_bytes=1024 * 1024),
        name="write_out",
    )(*results)


def solution(mesh):
    finer = Mesh(mesh.devices.reshape(8, 8, 4, 2), ("y", "z", "x", "c"))
    dp, mp, owners = ("y", "z"), ("x", "c"), ("x", "c", "y", "z")
    in_specs = (P(dp, mp), P(dp, mp), P(mp, None), P(owners, None), P(owners, None))
    out_specs = (P(owners, None), P(owners, None), P(None, dp, mp))
    return jax.shard_map(
        on_device, mesh=finer, in_specs=in_specs, out_specs=out_specs, check_vma=False
    )
```
